512 devices in a mesh: row: 16 (over x, z_hi, core), col: 32 (over z_lo, y).
Axes of the slice: x: 4, y: 4, z: 16 (z_hi: 2, z_lo: 8; z = z_hi * 8 + z_lo), core: 2. Of those that a mesh axis runs over, the one named last changes fastest.
Arguments:
- density: float32 [8192, 8192], P('row', 'col'), may hold values from -0.4375 to 0.4375
- occupancy: int32 [64, 64], P('row', 'col'), may hold values from 0 to 1, as said below
Outputs:
- purified: float32 [8192, 8192], P('row', 'col')
The draws below stay inside these ranges and needn't reach their ends.
Inputs may be any that keep to these rules, and one draw needn't show every extreme that they name: `occupancy`: 1 marks an occupied 128 x 128 tile, 0 an empty one; every diagonal tile is occupied.
All inputs are finite; a program needn't handle non-finite values.
Results may differ from the reference program's by a relative error of at most 0.0001.
Values sent between devices are 32-bit elements; how exact they have to be, the bound alone decides.
No kernel may reach another device: no remote copies, remote signals or barrier semaphores. Data moves between devices by JAX's collectives and lax.ppermute only.
A program may use at most 64 MiB of HBM per device.

```python
import jax
import jax.numpy as jnp
from jax import lax

BLK = 512
TILE = 128
SECTIONS = 3
ORDER = 8192


def draw_occupancy(key, part):
    tiles = ORDER // TILE
    grid_rows = ORDER // BLK
    grid_cols = 2 * grid_rows
    level_key = jax.random.fold_in(key, 11)
    tile_key = jax.random.fold_in(key, 23)
    levels = jax.random.randint(level_key, (grid_rows, grid_cols), 1, 4)
    per_tile = jnp.repeat(jnp.repeat(levels, BLK // TILE, axis=0), BLK // 2 // TILE, axis=1)
    rolls = jax.random.randint(tile_key, (tiles, tiles), 0, 3)
    occupied = jnp.where(rolls < per_tile, 1, 0).astype(jnp.int32)
    diagonal_tiles = jnp.eye(tiles, dtype=jnp.int32)
    return jnp.maximum(occupied, diagonal_tiles)


def level_of(stream_key, shape, pieces, least, top_value):
    level, own = 1.0, jax.random.fold_in(stream_key, 6)
    for position, blocks in pieces:
        draws = jnp.exp(jax.random.uniform(jax.random.fold_in(own, position), (blocks,), jnp.float32, least / len(pieces), top_value / len(pieces)))
        level = level * jnp.repeat(draws, shape[position] // blocks).reshape([-1 if axis == position else 1 for axis in range(len(shape))])
    return level


def noise(own_key, dims, scale, most, pieces=(), held_as=jnp.bfloat16):
    level = level_of(own_key, dims, pieces, -0.22, 0.18) if pieces else 1.0
    array = jax.random.normal(own_key, dims, jnp.float32) * scale * level
    return jnp.minimum(jnp.maximum(array, -most), most).astype(held_as)


def setup_inputs(seed: int = 0) -> dict:
    seeds = jax.random.split(jax.random.key(seed), 3)
    density = noise(seeds[0], (ORDER, ORDER), (3 * BLK // 8) ** -0.5, 0.4375, ((0, 16), (1, 32)), jnp.float32)
    occupancy = draw_occupancy(jax.random.fold_in(seeds[2], 71), 0)
    return dict(density=density, occupancy=occupancy)


def expand(occupancy):
    wide = jnp.repeat(jnp.repeat(occupancy, TILE, axis=0), TILE, axis=1)
    return wide.astype(jnp.float32)


def windowed(left, right):
    block_count = ORDER // BLK
    left_grid = left.reshape(block_count, BLK, block_count, BLK)
    right_grid = right.reshape(block_count, BLK, ORDER)
    rows_index = jnp.arange(block_count)
    accum = jnp.zeros((block_count, BLK, ORDER), jnp.float32)
    for section_index in range(SECTIONS):
        diag_blocks = left_grid[rows_index, :, (rows_index + section_index) % block_count, :]
        shifted = jnp.roll(right_grid, -section_index, axis=0)
        accum = accum + jnp.einsum("rij,rjn->rin", diag_blocks, shifted, precision=lax.Precision.HIGHEST)
    return accum.reshape(ORDER, ORDER)


def reference(density, occupancy):
    mask = expand(occupancy)
    masked = density * mask
    square_term = windowed(masked, masked) * mask
    cube_term = windowed(masked, square_term) * mask
    return 3.0 * square_term - 2.0 * cube_term
```

```python
import jax
import jax.numpy as jnp
from jax import lax
from jax.sharding import PartitionSpec as P

NX, NY, NZ = 4, 4, 8


def coords():
    for x in range(NX):
        for zh in range(2):
            for core in range(2):
                for zl in range(NZ):
                    for y in range(NY):
                        yield x, zh, core, zl, y


def linear(x, zh, core, zl, y):
    return ((x * 2 + zh) * 2 + core) * (NZ * NY) + zl * NY + y


def move(value, rule):
    pairs = []
    for at in coords():
        to = rule(*at)
        if to is not None:
            pairs.append((linear(*at), linear(*to)))
    return lax.ppermute(value, ("row", "col"), pairs)


def half_of(x, zh, core, zl, y):
    row = (x * 2 + zh) * 2 + core
    return (zl * NY + y - 2 * row) % (NZ * NY)


def owner(*at):
    return half_of(*at) < 6


def prev_group(x, zh):
    q = (x * 2 + zh - 1) % (2 * NX)
    return q // 2, q % 2


def tile_mask(values, occupancy):
    row_total, col_total = values.shape
    tile_rows, tile_cols = occupancy.shape
    shaped = values.reshape(tile_rows, row_total // tile_rows, tile_cols, col_total // tile_cols)
    weights = occupancy.astype(jnp.float32)[:, None, :, None]
    return (shaped * weights).reshape(row_total, col_total)


def after(value, other):
    return lax.optimization_barrier((value, other))[0]


def per_device(density, occupancy):
    row, col = lax.axis_index("row"), lax.axis_index("col")
    core, zh = row % 2, (row // 2) % 2
    zl, y = col // NY, col % NY
    masked = tile_mask(density, occupancy)

    def from_plane(flip, known):
        def rule(x, zh, core, zl, y):
            for mask in known:
                if owner(x, zh, core, zl ^ mask, y):
                    return x, zh, core, zl ^ flip, y
            return None

        return rule

    is_owner = (col - 2 * row) % (NZ * NY) < 6
    is_owner4 = ((zl ^ 4) * NY + y - 2 * row) % (NZ * NY) < 6
    got = move(masked, from_plane(4, (0,)))
    held = jnp.where(is_owner, masked, got)
    got = move(held, from_plane(2, (0, 4)))
    held = jnp.where(is_owner | is_owner4, held, got)
    got = move(held, from_plane(1, (0, 4, 2, 6)))
    mine_full = (zl % 2) == ((zh + core) % 2)
    full = jnp.where(mine_full, held, got)
    part = jnp.where(mine_full, got, held)

    def far(x, zh, core, zl, y):
        return (*prev_group(x, zh), core, zl, y)

    def partner(x, zh, core, zl, y):
        return x, zh, 1 - core, zl, y

    def right_rows(value, anchor=None):
        two = move(value if anchor is None else after(value, anchor), far)
        one = move(jnp.where(core == 0, two, value), partner)
        return jnp.concatenate([value, one, two])

    right = right_rows(masked, got)

    def along(step):
        return lambda x, zh, core, zl, y: (x, zh, core, zl, (y + step) % NY)

    def swap(x, zh, core, zl, y):
        return x, zh, core, zl, y ^ 1

    def part_out(x, zh, core, zl, y):
        return (x, zh, core, zl, 3 - y) if y // 2 == core else None

    def part_swap(x, zh, core, zl, y):
        return (x, zh, core, zl, y ^ 1) if y // 2 == core else None

    def part_over(x, zh, core, zl, y):
        return (x, zh, core, zl, 3 - y) if y // 2 == core else None

    below = move(full, along(1))
    above = move(full, along(-1))
    part_a = move(part, part_out)
    part_b = move(part, part_swap)
    across = move(jnp.where(y % 2 == 0, below, above), swap)
    part_c = move(part_b, part_over)
    has_part = (y // 2) == core
    part_near = jnp.where(has_part, part, part_a)
    part_far = jnp.where(has_part, part_b, part_c)
    near_y = jnp.where(has_part, y, 3 - y)

    full_of = lambda who: who % NY + 2 * core
    part_of = lambda who: jnp.where(core == 0, 4 + who, who - 2)
    lefts = [
        (full, full_of(y)),
        (below, full_of(y + NY - 1)),
        (above, full_of(y + 1)),
        (across, full_of(y + 2)),
        (part_near, part_of(near_y)),
        (part_far, part_of(near_y ^ 1)),
    ]

    def windowed(right):
        width = right.shape[1]
        accum = 0.0
        for left, half in lefts:
            rows = lax.dynamic_slice(right, (half * width, 0), (width, width))
            accum = accum + jnp.dot(
                left, rows, precision=lax.Precision.HIGHEST, preferred_element_type=jnp.float32
            )
        return accum

    square_term = tile_mask(windowed(right), occupancy)
    cube_term = tile_mask(windowed(right_rows(square_term)), occupancy)
    return 3.0 * square_term - 2.0 * cube_term


def solution(mesh):
    spec = P("row", "col")
    return jax.shard_map(
        per_device, mesh=mesh, in_specs=(spec, spec), out_specs=spec, check_vma=False
    )
```

```python
import jax
import jax.numpy as jnp
from jax import lax
from jax.sharding import PartitionSpec as P

NX, NY, NZ = 4, 4, 8


def coords():
    for x in range(NX):
        for zh in range(2):
            for core in range(2):
                for zl in range(NZ):
                    for y in range(NY):
                        yield x, zh, core, zl, y


def linear(x, zh, core, zl, y):
    return ((x * 2 + zh) * 2 + core) * (NZ * NY) + zl * NY + y


def move(value, rule):
    pairs = []
    for at in coords():
        to = rule(*at)
        if to is not None:
            pairs.append((linear(*at), linear(*to)))
    return lax.ppermute(value, ("row", "col"), pairs)


def half_of(x, zh, core, zl, y):
    row = (x * 2 + zh) * 2 + core
    return (zl * NY + y - 2 * row) % (NZ * NY)


def owner(*at):
    return half_of(*at) < 6


def prev_group(x, zh):
    q = (x * 2 + zh - 1) % (2 * NX)
    return q // 2, q % 2


def tile_mask(values, occupancy):
    row_total, col_total = values.shape
    tile_rows, tile_cols = occupancy.shape
    shaped = values.reshape(tile_rows, row_total // tile_rows, tile_cols, col_total // tile_cols)
    weights = occupancy.astype(jnp.float32)[:, None, :, None]
    return (shaped * weights).reshape(row_total, col_total)


def after(value, other):
    return lax.optimization_barrier((value, other))[0]


def per_device(density, occupancy):
    row, col = lax.axis_index("row"), lax.axis_index("col")
    core, zh = row % 2, (row // 2) % 2
    zl, y = col // NY, col % NY
    masked = tile_mask(density, occupancy)

    def from_plane(flip, known):
        def rule(x, zh, core, zl, y):
            for mask in known:
                if owner(x, zh, core, zl ^ mask, y):
                    return x, zh, core, zl ^ flip, y
            return None

        return rule

    is_owner = (col - 2 * row) % (NZ * NY) < 6
    is_owner4 = ((zl ^ 4) * NY + y - 2 * row) % (NZ * NY) < 6
    got = move(masked, from_plane(4, (0,)))
    held = jnp.where(is_owner, masked, got)
    got = move(held, from_plane(2, (0, 4)))
    held = jnp.where(is_owner | is_owner4, held, got)
    got = move(held, from_plane(1, (0, 4, 2, 6)))
    mine_full = (zl % 2) == ((zh + core) % 2)
    full = jnp.where(mine_full, held, got)
    part = jnp.where(mine_full, got, held)

    def far(x, zh, core, zl, y):
        return (*prev_group(x, zh), core, zl, y)

    def partner(x, zh, core, zl, y):
        return x, zh, 1 - core, zl, y

    def right_rows(value, two):
        one = move(jnp.where(core == 0, two, value), partner)
        return jnp.concatenate([value, one, two])

    masked_two = move(after(masked, got), far)

    def along(step):
        return lambda x, zh, core, zl, y: (x, zh, core, zl, (y + step) % NY)

    def swap(x, zh, core, zl, y):
        return x, zh, core, zl, y ^ 1

    def part_out(x, zh, core, zl, y):
        return (x, zh, core, zl, 3 - y) if y // 2 == core else None

    def part_swap(x, zh, core, zl, y):
        return (x, zh, core, zl, y ^ 1) if y // 2 == core else None

    def part_over(x, zh, core, zl, y):
        return (x, zh, core, zl, 3 - y) if y // 2 == core else None

    below = move(full, along(1))
    above = move(full, along(-1))
    part_a = move(part, part_out)
    part_b = move(part, part_swap)
    across = move(jnp.where(y % 2 == 0, below, above), swap)
    part_c = move(part_b, part_over)
    right = right_rows(masked, after(masked_two, (across, part_a, part_c)))
    has_part = (y // 2) == core
    part_near = jnp.where(has_part, part, part_a)
    part_far = jnp.where(has_part, part_b, part_c)
    near_y = jnp.where(has_part, y, 3 - y)

    full_of = lambda who: who % NY + 2 * core
    part_of = lambda who: jnp.where(core == 0, 4 + who, who - 2)
    lefts = [
        (full, full_of(y)),
        (below, full_of(y + NY - 1)),
        (above, full_of(y + 1)),
        (across, full_of(y + 2)),
        (part_near, part_of(near_y)),
        (part_far, part_of(near_y ^ 1)),
    ]

    def windowed(right):
        width = right.shape[1]
        accum = 0.0
        for left, half in lefts:
            rows = lax.dynamic_slice(right, (half * width, 0), (width, width))
            accum = accum + jnp.dot(
                left, rows, precision=lax.Precision.HIGHEST, preferred_element_type=jnp.float32
            )
        return accum

    square_term = tile_mask(windowed(right), occupancy)
    cube_term = tile_mask(windowed(right_rows(square_term, move(square_term, far))), occupancy)
    return 3.0 * square_term - 2.0 * cube_term


def solution(mesh):
    spec = P("row", "col")
    return jax.shard_map(
        per_device, mesh=mesh, in_specs=(spec, spec), out_specs=spec, check_vma=False
    )
```

```python
import jax
import jax.numpy as jnp
from jax import lax
from jax.sharding import PartitionSpec as P


NX, NY, NZ = 4, 4, 8


def coords():
    for x in range(NX):
        for zh in range(2):
            for core in range(2):
                for zl in range(NZ):
                    for y in range(NY):
                        yield x, zh, core, zl, y


def linear(x, zh, core, zl, y):
    return ((x * 2 + zh) * 2 + core) * (NZ * NY) + zl * NY + y


def move(value, rule):
    pairs = []
    for at in coords():
        to = rule(*at)
        if to is not None:
            pairs.append((linear(*at), linear(*to)))
    return lax.ppermute(value, ("row", "col"), pairs)


def half_of(x, zh, core, zl, y):
    row = (x * 2 + zh) * 2 + core
    return (zl * NY + y - 2 * row) % (NZ * NY)


def owner(*at):
    return half_of(*at) < 6


def prev_group(x, zh):
    q = (x * 2 + zh - 1) % (2 * NX)
    return q // 2, q % 2


def tile_mask(values, occupancy):
    row_total, col_total = values.shape
    tile_rows, tile_cols = occupancy.shape
    shaped = values.reshape(tile_rows, row_total // tile_rows, tile_cols, col_total // tile_cols)
    weights = occupancy.astype(jnp.float32)[:, None, :, None]
    return (shaped * weights).reshape(row_total, col_total)


def after(value, other):
    return lax.optimization_barrier((value, other))[0]


def per_device(density, occupancy):
    row, col = lax.axis_index("row"), lax.axis_index("col")
    core, zh = row % 2, (row // 2) % 2
    zl, y = col // NY, col % NY
    masked = tile_mask(density, occupancy)

    def from_plane(flip, known):
        def rule(x, zh, core, zl, y):
            for mask in known:
                if owner(x, zh, core, zl ^ mask, y):
                    return x, zh, core, zl ^ flip, y
            return None

        return rule

    is_owner = (col - 2 * row) % (NZ * NY) < 6
    is_owner4 = ((zl ^ 4) * NY + y - 2 * row) % (NZ * NY) < 6
    got = move(masked, from_plane(4, (0,)))
    held = jnp.where(is_owner, masked, got)
    got = move(held, from_plane(2, (0, 4)))
    held = jnp.where(is_owner | is_owner4, held, got)
    got = move(held, from_plane(1, (0, 4, 2, 6)))
    mine_full = (zl % 2) == ((zh + core) % 2)
    full = jnp.where(mine_full, held, got)
    part = jnp.where(mine_full, got, held)

    def far(x, zh, core, zl, y):
        return (*prev_group(x, zh), core, zl, y)

    def partner_of(which):
        return lambda x, zh, core, zl, y: (x, zh, 1 - core, zl, y) if core == which else None

    def along(step):
        return lambda x, zh, core, zl, y: (x, zh, core, zl, (y + step) % NY)

    def swap(x, zh, core, zl, y):
        return x, zh, core, zl, y ^ 1

    def part_swap(x, zh, core, zl, y):
        return (x, zh, core, zl, y ^ 1) if y // 2 == core else None

    def part_over(x, zh, core, zl, y):
        return (x, zh, core, zl, 3 - y) if y // 2 == core else None

    below = move(full, along(1))
    above = move(full, along(-1))
    masked_two = move(after(masked, got), far)
    part_b = move(part, part_swap)
    part_a = move(part, part_over)
    across = move(jnp.where(y % 2 == 0, below, above), swap)
    part_c = move(part_b, part_over)
    has_part = (y // 2) == core
    part_near = jnp.where(has_part, part, part_a)
    part_far = jnp.where(has_part, part_b, part_c)
    near_even = jnp.where(has_part, y, 3 - y) % 2 == 0

    size = full.shape[0]
    ring = jnp.concatenate([full, above, across, below, full, above, across])
    ring = lax.dynamic_slice(ring, ((NY - y) % NY * size, 0), (NY * size, ring.shape[1]))
    pair = jnp.concatenate(
        [jnp.where(near_even, part_near, part_far), jnp.where(near_even, part_far, part_near)]
    )
    panel = jnp.concatenate([pair, ring, pair])
    start = jnp.where(core == 0, 2 * size, 0)
    panel = lax.dynamic_slice(panel, (start, 0), (6 * size, ring.shape[1]))

    def product(section, rows):
        width = rows.shape[1]
        accum = 0.0
        for half in range(2):
            left = panel[(2 * section + half) * size : (2 * section + half + 1) * size]
            accum = accum + jnp.dot(
                left,
                rows[half * width : (half + 1) * width],
                precision=lax.Precision.HIGHEST,
                preferred_element_type=jnp.float32,
            )
        return accum

    def windowed(value, two, ready):
        from_one = move(value, partner_of(1))
        accum, from_one = lax.optimization_barrier((product(0, value), from_one))
        two = after(two, (accum, from_one, ready))
        from_zero = move(two, partner_of(0))
        accum = accum + product(2, two)
        one = jnp.where(core == 0, from_one, from_zero)
        return accum + product(1, one)

    square_term = tile_mask(windowed(masked, masked_two, (panel,)), occupancy)
    cube_two = move(square_term, far)
    cube_term = tile_mask(windowed(square_term, cube_two, ()), occupancy)
    return 3.0 * square_term - 2.0 * cube_term


def solution(mesh):
    spec = P("row", "col")
    return jax.shard_map(
        per_device, mesh=mesh, in_specs=(spec, spec), out_specs=spec, check_vma=False
    )
```

```python
import jax
import jax.numpy as jnp
from jax import lax
from jax.experimental import pallas as pl
from jax.experimental.pallas import tpu as pltpu
from jax.sharding import PartitionSpec as P


NX, NY, NZ = 4, 4, 8


def coords():
    for x in range(NX):
        for zh in range(2):
            for core in range(2):
                for zl in range(NZ):
                    for y in range(NY):
                        yield x, zh, core, zl, y


def linear(x, zh, core, zl, y):
    return ((x * 2 + zh) * 2 + core) * (NZ * NY) + zl * NY + y


def move(value, rule):
    pairs = []
    for at in coords():
        to = rule(*at)
        if to is not None:
            pairs.append((linear(*at), linear(*to)))
    return lax.ppermute(value, ("row", "col"), pairs)


def half_of(x, zh, core, zl, y):
    row = (x * 2 + zh) * 2 + core
    return (zl * NY + y - 2 * row) % (NZ * NY)


def owner(*at):
    return half_of(*at) < 6


def prev_group(x, zh):
    q = (x * 2 + zh - 1) % (2 * NX)
    return q // 2, q % 2


def tile_mask(values, occupancy):
    row_total, col_total = values.shape
    tile_rows, tile_cols = occupancy.shape
    shaped = values.reshape(tile_rows, row_total // tile_rows, tile_cols, col_total // tile_cols)
    weights = occupancy.astype(jnp.float32)[:, None, :, None]
    return (shaped * weights).reshape(row_total, col_total)


def split(value):
    high = value.astype(jnp.bfloat16)
    return high, (value - high.astype(jnp.float32)).astype(jnp.bfloat16)


def section_kernel(first, count, has_accum, finish, *refs):
    refs = list(refs)
    halves = refs.pop(0)
    occupancy = refs.pop(0) if finish else None
    rows = [refs.pop(0) for _ in range(count)]
    accum = refs.pop(0) if has_accum else None
    square = refs.pop(0) if finish == "cube" else None
    low, high, out = refs.pop(), refs.pop(), refs.pop()
    size, width = out.shape
    for index, block in enumerate(rows):
        high[index * size : (index + 1) * size], low[index * size : (index + 1) * size] = split(
            block[...]
        )
    out[...] = accum[...] if has_accum else jnp.zeros_like(out)
    for index, left in enumerate(refs):
        at = halves[index] - 2 * first

        @pl.when((at >= 0) & (at < 2 * count))
        def _():
            left_high, left_low = split(left[...])
            window = pl.ds(pl.multiple_of(at * width, width), width)
            right_high, right_low = high[window, :], low[window, :]
            dot = lambda p, q: jnp.dot(p, q, preferred_element_type=jnp.float32)
            out[...] += (dot(left_low, right_high) + dot(left_high, right_low)) + dot(
                left_high, right_high
            )

    if finish:
        tile_rows, tile_cols = size // 4, width // 2
        for i in range(4):
            for j in range(2):
                spot = (pl.ds(i * tile_rows, tile_rows), pl.ds(j * tile_cols, tile_cols))
                masked = out[spot] * occupancy[i, j].astype(jnp.float32)
                out[spot] = masked if square is None else 3.0 * square[spot] - 2.0 * masked


def section_product(lefts, halves, first, rows, accum=None, finish=None, occupancy=None, square=None):
    shape = rows[0].shape
    operands = [halves] + ([occupancy] if finish else []) + list(rows)
    operands += ([] if accum is None else [accum]) + ([square] if finish == "cube" else [])
    operands += list(lefts)
    smem = 2 if finish else 1
    in_specs = [pl.BlockSpec(memory_space=pltpu.SMEM)] * smem
    in_specs += [pl.BlockSpec(memory_space=pltpu.VMEM)] * (len(operands) - smem)
    pieces = pltpu.VMEM((len(rows) * shape[0], shape[1]), jnp.bfloat16)

    def body(*refs):
        section_kernel(first, len(rows), accum is not None, finish, *refs)

    return pl.pallas_call(
        body,
        out_shape=jax.ShapeDtypeStruct(shape, jnp.float32),
        in_specs=in_specs,
        out_specs=pl.BlockSpec(memory_space=pltpu.VMEM),
        scratch_shapes=[pieces, pieces],
        compiler_params=pltpu.CompilerParams(vmem_limit_bytes=24 << 20),
        cost_estimate=pl.CostEstimate(
            flops=len(rows) * 6 * 2 * shape[0] * shape[1] * shape[1],
            bytes_accessed=8 * shape[0] * shape[1],
            transcendentals=0,
        ),
    )(*operands)


def after(value, other):
    return lax.optimization_barrier((value, other))[0]


def per_device(density, occupancy):
    row, col = lax.axis_index("row"), lax.axis_index("col")
    core, zh = row % 2, (row // 2) % 2
    zl, y = col // NY, col % NY
    masked = tile_mask(density, occupancy)

    def from_plane(flip, known):
        def rule(x, zh, core, zl, y):
            for mask in known:
                if owner(x, zh, core, zl ^ mask, y):
                    return x, zh, core, zl ^ flip, y
            return None

        return rule

    is_owner = (col - 2 * row) % (NZ * NY) < 6
    is_owner4 = ((zl ^ 4) * NY + y - 2 * row) % (NZ * NY) < 6
    got = move(masked, from_plane(4, (0,)))
    held = jnp.where(is_owner, masked, got)
    got = move(held, from_plane(2, (0, 4)))
    held = jnp.where(is_owner | is_owner4, held, got)

    def holds_full(zh, core, zl):
        return zl % 2 == (zh + core) % 2

    def spread(value, own):
        def rule_of(full_rule, part_rule):
            def rule(x, zh, core, zl, y):
                if holds_full(zh, core, zl) == own:
                    to = full_rule(y)
                else:
                    to = part_rule(y) if y // 2 == core else None
                return None if to is None else (x, zh, core, zl, to % NY)

            return rule

        one = move(value, rule_of(lambda y: y + 1, lambda y: y ^ 1))
        two = move(value, rule_of(lambda y: y - 1, lambda y: 3 - y))
        is_full = mine_full if own else ~mine_full
        on = jnp.where(is_full & (y % 2 == 1), two, one)
        return one, two, move(on, rule_of(lambda y: y ^ 1, lambda y: 3 - y))

    def kinds(own):
        is_full = mine_full if own else ~mine_full
        as_full = [(y + step) % NY + 2 * core for step in (0, NY - 1, 1, 2)]
        has_part = (y // 2) == core
        part_of = lambda who: jnp.where(core == 0, 4 + who, who - 2)
        as_part = [
            jnp.where(has_part, part_of(y), -1),
            jnp.where(has_part, part_of(y ^ 1), -1),
            jnp.where(has_part, -1, part_of(3 - y)),
            jnp.where(has_part, -1, part_of((3 - y) ^ 1)),
        ]
        return [jnp.where(is_full, f, p) for f, p in zip(as_full, as_part)]

    mine_full = holds_full(zh, core, zl)
    got = move(held, from_plane(1, (0, 4, 2, 6)))
    own_moved = spread(held, True)

    def far(x, zh, core, zl, y):
        return (*prev_group(x, zh), core, zl, y)

    def partner_of(which):
        return lambda x, zh, core, zl, y: (x, zh, 1 - core, zl, y) if core == which else None

    masked_two = move(after(masked, got), far)
    other_moved = spread(got, False)

    lefts = [held, *own_moved, got, *other_moved]
    halves = jnp.stack(kinds(True) + kinds(False)).astype(jnp.int32)
    section = halves // 2
    early = jnp.where((section == 0) | ((core == 0) & (section == 1)), halves, -1)
    late = jnp.where((core == 1) & (section == 1), halves, -1)

    def windowed(value, two, finish, square=None):
        from_one = move(value, partner_of(1))
        accum = section_product(lefts, early, 0, [value, from_one])
        two, accum = lax.optimization_barrier((two, accum))
        from_zero = move(two, partner_of(0))
        accum = section_product(lefts, halves, 2, [two], accum)
        return section_product(lefts, late, 1, [from_zero], accum, finish, occupancy, square)

    square_term = windowed(masked, masked_two, "square")
    cube_two = move(square_term, far)
    return windowed(square_term, cube_two, "cube", square_term)


def solution(mesh):
    spec = P("row", "col")
    return jax.shard_map(
        per_device, mesh=mesh, in_specs=(spec, spec), out_specs=spec, check_vma=False
    )
```

```python
import jax
import jax.numpy as jnp
from jax import lax
from jax.experimental import pallas as pl
from jax.experimental.pallas import tpu as pltpu
from jax.sharding import PartitionSpec as P


NX, NY, NZ = 4, 4, 8


def coords():
    for x in range(NX):
        for zh in range(2):
            for core in range(2):
                for zl in range(NZ):
                    for y in range(NY):
                        yield x, zh, core, zl, y


def linear(x, zh, core, zl, y):
    return ((x * 2 + zh) * 2 + core) * (NZ * NY) + zl * NY + y


def move(value, rule):
    pairs = []
    for at in coords():
        to = rule(*at)
        if to is not None:
            pairs.append((linear(*at), linear(*to)))
    return lax.ppermute(value, ("row", "col"), pairs)


def half_of(x, zh, core, zl, y):
    row = (x * 2 + zh) * 2 + core
    return (zl * NY + y - 2 * row) % (NZ * NY)


def owner(*at):
    return half_of(*at) < 6


def prev_group(x, zh):
    q = (x * 2 + zh - 1) % (2 * NX)
    return q // 2, q % 2


def tile_mask(values, occupancy):
    row_total, col_total = values.shape
    tile_rows, tile_cols = occupancy.shape
    shaped = values.reshape(tile_rows, row_total // tile_rows, tile_cols, col_total // tile_cols)
    weights = occupancy.astype(jnp.float32)[:, None, :, None]
    return (shaped * weights).reshape(row_total, col_total)


def split(value):
    high = value.astype(jnp.bfloat16)
    return high, (value - high.astype(jnp.float32)).astype(jnp.bfloat16)


def section_kernel(first, count, has_accum, finish, *refs):
    refs = list(refs)
    halves = refs.pop(0)
    occupancy = refs.pop(0) if finish else None
    rows = [refs.pop(0) for _ in range(count)]
    accum = refs.pop(0) if has_accum else None
    square = refs.pop(0) if finish == "cube" else None
    low, high, out = refs.pop(), refs.pop(), refs.pop()
    size, width = out.shape
    for index, block in enumerate(rows):
        high[index * size : (index + 1) * size], low[index * size : (index + 1) * size] = split(
            block[...]
        )
    out[...] = accum[...] if has_accum else jnp.zeros_like(out)
    for index, left in enumerate(refs):
        at = halves[index] - 2 * first

        @pl.when((at >= 0) & (at < 2 * count))
        def _():
            left_high, left_low = split(left[...])
            window = pl.ds(pl.multiple_of(at * width, width), width)
            right_high, right_low = high[window, :], low[window, :]
            dot = lambda p, q: jnp.dot(p, q, preferred_element_type=jnp.float32)
            out[...] += (dot(left_low, right_high) + dot(left_high, right_low)) + dot(
                left_high, right_high
            )

    if finish:
        tile_rows, tile_cols = size // 4, width // 2
        for i in range(4):
            for j in range(2):
                spot = (pl.ds(i * tile_rows, tile_rows), pl.ds(j * tile_cols, tile_cols))
                masked = out[spot] * occupancy[i, j].astype(jnp.float32)
                out[spot] = masked if square is None else 3.0 * square[spot] - 2.0 * masked


def section_product(lefts, halves, first, rows, accum=None, finish=None, occupancy=None, square=None):
    shape = rows[0].shape
    operands = [halves] + ([occupancy] if finish else []) + list(rows)
    operands += ([] if accum is None else [accum]) + ([square] if finish == "cube" else [])
    operands += list(lefts)
    smem = 2 if finish else 1
    in_specs = [pl.BlockSpec(memory_space=pltpu.SMEM)] * smem
    in_specs += [pl.BlockSpec(memory_space=pltpu.VMEM)] * (len(operands) - smem)
    pieces = pltpu.VMEM((len(rows) * shape[0], shape[1]), jnp.bfloat16)

    def body(*refs):
        section_kernel(first, len(rows), accum is not None, finish, *refs)

    return pl.pallas_call(
        body,
        out_shape=jax.ShapeDtypeStruct(shape, jnp.float32),
        in_specs=in_specs,
        out_specs=pl.BlockSpec(memory_space=pltpu.VMEM),
        scratch_shapes=[pieces, pieces],
        compiler_params=pltpu.CompilerParams(vmem_limit_bytes=6 << 20),
        cost_estimate=pl.CostEstimate(
            flops=len(rows) * 6 * 2 * shape[0] * shape[1] * shape[1],
            bytes_accessed=8 * shape[0] * shape[1],
            transcendentals=0,
        ),
    )(*operands)


def per_device(density, occupancy):
    row, col = lax.axis_index("row"), lax.axis_index("col")
    core, zh = row % 2, (row // 2) % 2
    zl, y = col // NY, col % NY
    masked = tile_mask(density, occupancy)

    def from_plane(flip, known):
        def rule(x, zh, core, zl, y):
            for mask in known:
                if owner(x, zh, core, zl ^ mask, y):
                    return x, zh, core, zl ^ flip, y
            return None

        return rule

    is_owner = (col - 2 * row) % (NZ * NY) < 6
    is_owner4 = ((zl ^ 4) * NY + y - 2 * row) % (NZ * NY) < 6
    got = move(masked, from_plane(4, (0,)))
    held = jnp.where(is_owner, masked, got)
    got = move(held, from_plane(2, (0, 4)))
    held = jnp.where(is_owner | is_owner4, held, got)

    def holds_full(zh, core, zl):
        return zl % 2 == (zh + core) % 2

    def spread(value, own):
        def rule_of(full_rule, part_rule):
            def rule(x, zh, core, zl, y):
                if holds_full(zh, core, zl) == own:
                    to = full_rule(y)
                else:
                    to = part_rule(y) if y // 2 == core else None
                return None if to is None else (x, zh, core, zl, to % NY)

            return rule

        one = move(value, rule_of(lambda y: y + 1, lambda y: y ^ 1))
        two = move(value, rule_of(lambda y: y - 1, lambda y: 3 - y))
        is_full = mine_full if own else ~mine_full
        on = jnp.where(is_full & (y % 2 == 1), two, one)
        return one, two, move(on, rule_of(lambda y: y ^ 1, lambda y: 3 - y))

    def kinds(own):
        is_full = mine_full if own else ~mine_full
        as_full = [(y + step) % NY + 2 * core for step in (0, NY - 1, 1, 2)]
        has_part = (y // 2) == core
        part_of = lambda who: jnp.where(core == 0, 4 + who, who - 2)
        as_part = [
            jnp.where(has_part, part_of(y), -1),
            jnp.where(has_part, part_of(y ^ 1), -1),
            jnp.where(has_part, -1, part_of(3 - y)),
            jnp.where(has_part, -1, part_of((3 - y) ^ 1)),
        ]
        return [jnp.where(is_full, f, p) for f, p in zip(as_full, as_part)]

    mine_full = holds_full(zh, core, zl)
    got = move(held, from_plane(1, (0, 4, 2, 6)))
    own_moved = spread(held, True)

    def far(x, zh, core, zl, y):
        return (*prev_group(x, zh), core, zl, y)

    def partner_of(which):
        return lambda x, zh, core, zl, y: (x, zh, 1 - core, zl, y) if core == which else None

    masked_two = move(masked, far)
    other_moved = spread(got, False)

    lefts = [held, *own_moved, got, *other_moved]
    halves = jnp.stack(kinds(True) + kinds(False)).astype(jnp.int32)
    section = halves // 2
    early = jnp.where((section == 0) | ((core == 0) & (section == 1)), halves, -1)
    late = jnp.where((core == 1) & (section == 1), halves, -1)

    def windowed(value, two, finish, square=None):
        from_one = move(value, partner_of(1))
        accum = section_product(lefts, early, 0, [value, from_one])
        from_zero = move(two, partner_of(0))
        accum = section_product(lefts, halves, 2, [two], accum)
        return section_product(lefts, late, 1, [from_zero], accum, finish, occupancy, square)

    square_term = windowed(masked, masked_two, "square")
    cube_two = move(square_term, far)
    return windowed(square_term, cube_two, "cube", square_term)


def solution(mesh):
    spec = P("row", "col")
    return jax.shard_map(
        per_device, mesh=mesh, in_specs=(spec, spec), out_specs=spec, check_vma=False
    )
```

```python
import jax
import jax.numpy as jnp
from jax import lax
from jax.experimental import pallas as pl
from jax.experimental.pallas import tpu as pltpu
from jax.sharding import PartitionSpec as P


NX, NY, NZ = 4, 4, 8


def coords():
    for x in range(NX):
        for zh in range(2):
            for core in range(2):
                for zl in range(NZ):
                    for y in range(NY):
                        yield x, zh, core, zl, y


def linear(x, zh, core, zl, y):
    return ((x * 2 + zh) * 2 + core) * (NZ * NY) + zl * NY + y


def move(value, rule):
    pairs = []
    for at in coords():
        to = rule(*at)
        if to is not None:
            pairs.append((linear(*at), linear(*to)))
    return lax.ppermute(value, ("row", "col"), pairs)


def half_of(x, zh, core, zl, y):
    row = (x * 2 + zh) * 2 + core
    return (zl * NY + y - 2 * row) % (NZ * NY)


def owner(*at):
    return half_of(*at) < 6


def prev_group(x, zh):
    q = (x * 2 + zh - 1) % (2 * NX)
    return q // 2, q % 2


def tile_mask(values, occupancy):
    row_total, col_total = values.shape
    tile_rows, tile_cols = occupancy.shape
    shaped = values.reshape(tile_rows, row_total // tile_rows, tile_cols, col_total // tile_cols)
    weights = occupancy.astype(jnp.float32)[:, None, :, None]
    return (shaped * weights).reshape(row_total, col_total)


def split(value):
    high = value.astype(jnp.bfloat16)
    return high, (value - high.astype(jnp.float32)).astype(jnp.bfloat16)


def section_kernel(first, count, has_accum, finish, *refs):
    refs = list(refs)
    halves = refs.pop(0)
    occupancy = refs.pop(0) if finish else None
    rows = [refs.pop(0) for _ in range(count)]
    accum = refs.pop(0) if has_accum else None
    square = refs.pop(0) if finish == "cube" else None
    right, out = refs.pop(), refs.pop()
    size, width = out.shape
    for index, block in enumerate(rows):
        for half in range(2):
            upper, lower = split(block[half * width : (half + 1) * width])
            for piece, part in enumerate((upper, lower, upper)):
                right[2 * index + half, piece * width : (piece + 1) * width] = part
    out[...] = accum[...] if has_accum else jnp.zeros_like(out)
    for index, left in enumerate(refs):
        at = halves[index] - 2 * first

        @pl.when((at >= 0) & (at < 2 * count))
        def _():
            upper, lower = split(left[...])
            pieces = jnp.concatenate([lower, upper, upper], axis=1)
            out[...] += jnp.dot(pieces, right[at], preferred_element_type=jnp.float32)

    if finish:
        tile_rows, tile_cols = size // 4, width // 2
        for i in range(4):
            for j in range(2):
                spot = (pl.ds(i * tile_rows, tile_rows), pl.ds(j * tile_cols, tile_cols))
                masked = out[spot] * occupancy[i, j].astype(jnp.float32)
                out[spot] = masked if square is None else 3.0 * square[spot] - 2.0 * masked


def section_product(lefts, halves, first, rows, accum=None, finish=None, occupancy=None, square=None):
    shape = rows[0].shape
    operands = [halves] + ([occupancy] if finish else []) + list(rows)
    operands += ([] if accum is None else [accum]) + ([square] if finish == "cube" else [])
    operands += list(lefts)
    smem = 2 if finish else 1
    in_specs = [pl.BlockSpec(memory_space=pltpu.SMEM)] * smem
    in_specs += [pl.BlockSpec(memory_space=pltpu.VMEM)] * (len(operands) - smem)
    pieces = pltpu.VMEM((2 * len(rows), 3 * shape[1], shape[1]), jnp.bfloat16)

    def body(*refs):
        section_kernel(first, len(rows), accum is not None, finish, *refs)

    return pl.pallas_call(
        body,
        out_shape=jax.ShapeDtypeStruct(shape, jnp.float32),
        in_specs=in_specs,
        out_specs=pl.BlockSpec(memory_space=pltpu.VMEM),
        scratch_shapes=[pieces],
        compiler_params=pltpu.CompilerParams(vmem_limit_bytes=6 << 20),
        cost_estimate=pl.CostEstimate(
            flops=len(rows) * 6 * 2 * shape[0] * shape[1] * shape[1],
            bytes_accessed=8 * shape[0] * shape[1],
            transcendentals=0,
        ),
    )(*operands)


def per_device(density, occupancy):
    row, col = lax.axis_index("row"), lax.axis_index("col")
    core, zh = row % 2, (row // 2) % 2
    zl, y = col // NY, col % NY
    masked = tile_mask(density, occupancy)

    def from_plane(flip, known):
        def rule(x, zh, core, zl, y):
            for mask in known:
                if owner(x, zh, core, zl ^ mask, y):
                    return x, zh, core, zl ^ flip, y
            return None

        return rule

    is_owner = (col - 2 * row) % (NZ * NY) < 6
    is_owner4 = ((zl ^ 4) * NY + y - 2 * row) % (NZ * NY) < 6
    got = move(masked, from_plane(4, (0,)))
    held = jnp.where(is_owner, masked, got)
    got = move(held, from_plane(2, (0, 4)))
    held = jnp.where(is_owner | is_owner4, held, got)

    def holds_full(zh, core, zl):
        return zl % 2 == (zh + core) % 2

    def spread(value, own):
        def rule_of(full_rule, part_rule):
            def rule(x, zh, core, zl, y):
                if holds_full(zh, core, zl) == own:
                    to = full_rule(y)
                else:
                    to = part_rule(y) if y // 2 == core else None
                return None if to is None else (x, zh, core, zl, to % NY)

            return rule

        one = move(value, rule_of(lambda y: y + 1, lambda y: y ^ 1))
        two = move(value, rule_of(lambda y: y - 1, lambda y: 3 - y))
        is_full = mine_full if own else ~mine_full
        on = jnp.where(is_full & (y % 2 == 1), two, one)
        return one, two, move(on, rule_of(lambda y: y ^ 1, lambda y: 3 - y))

    def kinds(own):
        is_full = mine_full if own else ~mine_full
        as_full = [(y + step) % NY + 2 * core for step in (0, NY - 1, 1, 2)]
        has_part = (y // 2) == core
        part_of = lambda who: jnp.where(core == 0, 4 + who, who - 2)
        as_part = [
            jnp.where(has_part, part_of(y), -1),
            jnp.where(has_part, part_of(y ^ 1), -1),
            jnp.where(has_part, -1, part_of(3 - y)),
            jnp.where(has_part, -1, part_of((3 - y) ^ 1)),
        ]
        return [jnp.where(is_full, f, p) for f, p in zip(as_full, as_part)]

    mine_full = holds_full(zh, core, zl)
    got = move(held, from_plane(1, (0, 4, 2, 6)))
    own_moved = spread(held, True)

    def far(x, zh, core, zl, y):
        return (*prev_group(x, zh), core, zl, y)

    def partner_of(which):
        return lambda x, zh, core, zl, y: (x, zh, 1 - core, zl, y) if core == which else None

    masked_two = move(masked, far)
    other_moved = spread(got, False)

    lefts = [held, *own_moved, got, *other_moved]
    halves = jnp.stack(kinds(True) + kinds(False)).astype(jnp.int32)
    section = halves // 2
    early = jnp.where((section == 0) | ((core == 0) & (section == 1)), halves, -1)
    late = jnp.where((core == 1) & (section == 1), halves, -1)

    def windowed(value, two, finish, square=None):
        from_one = move(value, partner_of(1))
        accum = section_product(lefts, early, 0, [value, from_one])
        from_zero = move(two, partner_of(0))
        accum = section_product(lefts, halves, 2, [two], accum)
        return section_product(lefts, late, 1, [from_zero], accum, finish, occupancy, square)

    square_term = windowed(masked, masked_two, "square")
    cube_two = move(square_term, far)
    return windowed(square_term, cube_two, "cube", square_term)


def solution(mesh):
    spec = P("row", "col")
    return jax.shard_map(
        per_device, mesh=mesh, in_specs=(spec, spec), out_specs=spec, check_vma=False
    )
```
